32 devices in a mesh: group: 2 (over y), beam: 4 (over z), fft: 2 (over x), sub: 2 (over core).
Axes of the slice: x: 2, y: 2, z: 4, core: 2. Of those that a mesh axis runs over, the one named last changes fastest.
Arguments:
- uv_grid: float32 [8, 2, 2048, 2048], P(('group', 'beam'), None, ('fft', 'sub')), parts along dimension 0, may hold values from -6 to 6
- beam_gain: float32 [8, 512, 512], P(('group', 'beam'), ('fft', 'sub')), parts along dimension 0, may hold values from 0.1 to 1
- sub_pixel: float32 [8, 2], P(('group', 'beam')), parts along dimension 0, may hold values from 0 to 1
- intersection_tiles: int32 [8, 4], P('group'), parts along dimension 0, may hold values from 0 to 7, as said below
- tile_offsets: int32 [8, 4, 2], P(('group', 'beam')), parts along dimension 0, may hold values from 0 to 252
Outputs:
- sky: float32 [16, 256, 256], P(('group', 'beam'), ('fft', 'sub')), parts along dimension 0
The draws below stay inside these ranges and needn't reach their ends.
There are 2 independent parts, one for each index of `group`. The reference program is written for one: setup_inputs(seed, part) draws one part's arguments, and reference() takes and returns one part's arrays. A program takes and returns all parts, laid end to end along the dimension named above; each array names one. Nothing has to cross between parts.
Inputs may be any that keep to these rules, and one draw needn't show every extreme that they name: `intersection_tiles`: each row names 4 distinct sky tiles; sky tile t belongs to owner t // 2, and the tiles of beam b belong to owners b - 1 to b + 2 taken modulo the number of owners, with at most 2 of them on one owner.
All inputs are finite; a program needn't handle non-finite values.
Results may differ from the reference program's by a relative error of at most 0.0037.
Values may be sent and summed in bfloat16 or wider, within the bound.
A program may use at most 64 MiB of HBM per device.

```python
import math
import jax
import jax.numpy as jnp
from jax import lax

NG = 2048
W = 512
S = 256
K = 4
TILE_DEV = 2
BEAMS = 4
TILES = 8


def draw_intersection_tiles(key, part):
    owners = TILES // TILE_DEV
    full = jax.random.randint(jax.random.fold_in(key, 11), (BEAMS,), 0, 4)
    keys = jax.random.split(jax.random.fold_in(key, 12), BEAMS)
    others = jax.vmap(lambda k: jax.random.permutation(k, 3 * TILE_DEV)[:K - TILE_DEV])(keys)
    others = others + TILE_DEV * (others >= TILE_DEV * full[:, None]).astype(jnp.int32)
    paired = full[:, None] * TILE_DEV + jnp.arange(TILE_DEV, dtype=jnp.int32)[None, :]
    nearby = jnp.concatenate([paired, others], axis=1).astype(jnp.int32)
    distance = nearby // TILE_DEV - 1
    beams = jnp.arange(BEAMS, dtype=jnp.int32)[:, None]
    holder = jnp.mod(beams + distance, owners)
    return (holder * TILE_DEV + jnp.mod(nearby, TILE_DEV)).astype(jnp.int32)


def set_ends(drawn, key, smallest, largest):
    spot = [jax.random.randint(jax.random.fold_in(key, axis), (), 0, length) for axis, length in enumerate(drawn.shape)]
    longest = drawn.shape.index(max(drawn.shape))
    next_to = spot[:longest] + [(spot[longest] + 1) % drawn.shape[longest]] + spot[longest + 1:]
    return drawn.at[tuple(spot)].set(smallest).at[tuple(next_to)].set(largest)


def levels(own_key, dims, cuts, smallest, largest):
    def one(position, shards_of):
        heights = jax.random.uniform(jax.random.fold_in(jax.random.fold_in(own_key, 6), position), (shards_of,), jnp.float32, smallest / len(cuts), largest / len(cuts))
        return jnp.repeat(jnp.exp(heights), dims[position] // shards_of).reshape((-1,) + (1,) * (len(dims) - position - 1))

    factor_of = one(*cuts[0])
    for cut in cuts[1:]:
        factor_of = factor_of * one(*cut)
    return factor_of


def scatter_about(stream_key, dims, scale, reach, cuts=(), kind=jnp.bfloat16):
    values = scale * jax.random.normal(stream_key, dims, jnp.float32)
    if cuts:
        values = values * levels(stream_key, dims, cuts, -0.22, 0.18)
    return jnp.clip(values, -reach, reach).astype(kind)


def setup_inputs(seed: int = 0, part: int = 0) -> dict:
    key_of = jax.random.split(jax.random.key(seed), 6)
    part_splits = jax.random.split(jax.random.fold_in(key_of[5], part), 6)
    uv_grid = scatter_about(part_splits[0], (BEAMS, 2, NG, NG), 1.0, 6.0, ((0, 4), (2, 4)), jnp.float32)
    beam_gain = jnp.clip(jnp.exp(math.log(1.0) - 2.3025851 * jax.random.uniform(part_splits[1], (BEAMS, W, W), jnp.float32) ** levels(part_splits[1], (BEAMS, W, W), ((0, 4), (1, 4)), -0.2, 0.2)), 0.1, 1.0)
    sub_pixel = jnp.clip(1.0 * jax.random.uniform(part_splits[2], (BEAMS, 2), jnp.float32) ** levels(part_splits[2], (BEAMS, 2), ((0, 4),), -0.2, 0.2), 0.0, 1.0)
    intersection_tiles = draw_intersection_tiles(jax.random.fold_in(jax.random.fold_in(key_of[5], part), 71), part)
    tile_offsets = set_ends(jax.random.randint(part_splits[4], (BEAMS, K, 2), 0, W - S - 3), jax.random.fold_in(part_splits[4], 1), 0, (W - S - 3) - 1).astype(jnp.int32)
    return dict(uv_grid=uv_grid, beam_gain=beam_gain, sub_pixel=sub_pixel, intersection_tiles=intersection_tiles, tile_offsets=tile_offsets)


def phase_table(rows, cols, length):
    turns = jnp.mod(rows[:, None] * cols[None, :], length)
    angle = turns.astype(jnp.float32) * (2.0 * 3.141592653589793 / length)
    return jnp.cos(angle), jnp.sin(angle)


def kernel_weight(t):
    a = jnp.abs(t)
    near = (1.5 * a - 2.5) * a * a + 1.0
    far = ((-0.5 * a + 2.5) * a - 4.0) * a + 2.0
    return jnp.where(a <= 1.0, near, jnp.where(a < 2.0, far, 0.0 * a))


def interp(offset, frac, rows, cols):
    place = (offset + 1 + rows).astype(frac.dtype) + frac
    return kernel_weight(cols.astype(frac.dtype)[None, :] - place[:, None])


def reference(uv_grid, beam_gain, sub_pixel, intersection_tiles, tile_offsets):
    half = W // 2
    sky_cols = (jnp.arange(W) - half).astype(jnp.int32)
    freq = jnp.arange(NG).astype(jnp.int32)
    cos_u, sin_u = phase_table(freq, sky_cols, NG)
    cos_b = cos_u.astype(jnp.bfloat16)
    sin_b = sin_u.astype(jnp.bfloat16)
    columns = jnp.mod(sky_cols, NG)
    tile_rows = jnp.arange(S).astype(jnp.int32)
    image_index = jnp.arange(W).astype(jnp.int32)

    def one_beam(items):
        grid, gain, shift, offsets = items
        field = lax.complex(grid[0], grid[1])
        spectra = jnp.fft.ifft(field, axis=1)[:, columns] * NG
        real_b = jnp.real(spectra).astype(jnp.bfloat16)
        imag_b = jnp.imag(spectra).astype(jnp.bfloat16)
        image = (jnp.dot(cos_b.T, real_b, preferred_element_type=jnp.float32)
                 - jnp.dot(sin_b.T, imag_b, preferred_element_type=jnp.float32)) / NG
        stacked = jnp.stack([gain * image, gain * gain])
        down = jax.vmap(lambda off: interp(off, shift[0], tile_rows, image_index))(offsets[:, 0])
        across = jax.vmap(lambda off: interp(off, shift[1], tile_rows, image_index))(offsets[:, 1])
        left = jnp.einsum('kiy,cyx->kcix', down, stacked, precision=lax.Precision.HIGHEST)
        return jnp.einsum('kcix,kjx->kcij', left, across, precision=lax.Precision.HIGHEST)

    pieces = lax.map(one_beam, (uv_grid, beam_gain, sub_pixel, tile_offsets))
    sums = jax.ops.segment_sum(pieces.reshape(BEAMS * K, 2, S, S), intersection_tiles.reshape(-1), num_segments=TILES)
    return sums[:, 0] / jnp.maximum(sums[:, 1], 0.5)
```

```python
import functools

import jax
import jax.numpy as jnp
import ml_dtypes
import numpy as np
from jax import lax
from jax.experimental import pallas as pl
from jax.experimental.pallas import tpu as pltpu
from jax.sharding import PartitionSpec as P

S = 256
TILE_DEV = 2
RADIX = 4
HOPS = (2, 1, -1)
PARTS = 2
LEVELS = 32000.0
LANES = 128
MESH = pl.DeviceIdType.MESH
F32 = jnp.float32
BF16 = jnp.bfloat16


def turns(rows, cols, length):
    angle = np.mod(np.outer(rows, cols), length) * (2.0 * np.pi / length)
    return np.cos(angle), np.sin(angle)


def column_tables(length, window):
    fold = length // RADIX
    per = window // RADIX
    tables = []
    for c in range(RADIX):
        cos, sin = turns(np.arange(fold), RADIX * np.arange(per) + c - window // 2, length)
        tables.append(np.concatenate([cos, sin], axis=1))
    full = np.stack(tables).astype(np.float32)
    high = full.astype(ml_dtypes.bfloat16)
    low = (full - high.astype(np.float32)).astype(ml_dtypes.bfloat16)
    return np.stack([high, low])


def row_tables(length, window, rows):
    cos, sin = turns(np.arange(window) - window // 2, np.arange(rows), length)
    return np.stack([cos, sin]).astype(np.float32).astype(ml_dtypes.bfloat16)


def near(a):
    return (1.5 * a - 2.5) * a * a + 1.0


def far(a):
    return ((-0.5 * a + 2.5) * a - 4.0) * a + 2.0


def taps(frac):
    return far(1.0 + frac), near(frac), near(1.0 - frac), far(2.0 - frac)


def kernel(
    quarter, step, shift_ref, tiles_ref, offs_ref, gain_hbm, uv_ref, col_hbm, row_hbm, out_ref,
    buf, col_ref, row_ref, table, spec, own, gall, filt, squares, mats, pieces, psend, precv,
    xsend, xrecv, zsend, zrecv, dsend, drecv,
    load_sems, gsems, grecv, csems, crecv, xsems, xrsems, zsems, zrsems, dsems, drsems,
):
    chip, core = lax.axis_index("fft"), lax.axis_index("sub")
    chips, cores = lax.axis_size("fft"), lax.axis_size("sub")
    me = chip * cores + core
    owner = lax.axis_index("beam")
    owners = lax.axis_size("beam")
    rows, length = buf.shape[1], buf.shape[2]
    fold = length // RADIX
    own_rows, window = own.shape
    per = window // RADIX
    side = pieces.shape[3]
    count = offs_ref.shape[2]
    chunks = rows // step
    parts = xsend.shape[0]
    cut = side // parts

    def load(i):
        span = pl.ds(pl.multiple_of(i * step, step), step)
        return pltpu.make_async_copy(uv_ref.at[0, :, span], buf.at[:, span], load_sems.at[i])

    gain_load = pltpu.make_async_copy(gain_hbm.at[0], own, load_sems.at[chunks])
    col_load = pltpu.make_async_copy(col_hbm, col_ref, load_sems.at[chunks + 1])
    row_load = pltpu.make_async_copy(row_hbm, row_ref, load_sems.at[chunks + 2])
    gain_load.start()
    col_load.start()
    for i in range(chunks):
        load(i).start()
    row_load.start()

    def beam(hop):
        return {"beam": lax.rem(owner + hop + owners, owners)}

    def at(a, e):
        other = lax.rem(chip + a + chips, chips), lax.rem(core + e + cores, cores)
        return {"fft": other[0], "sub": other[1]}, other[0] * cores + other[1]

    barrier = pltpu.get_barrier_semaphore()
    for a in range(chips):
        for e in range(cores):
            if a or e:
                pl.semaphore_signal(barrier, inc=1, device_id=at(a, e)[0], device_id_type=MESH)
    for hop in HOPS:
        pl.semaphore_signal(barrier, inc=1, device_id=beam(-hop), device_id_type=MESH)

    def remote(src, dst, send, recv, device):
        return pltpu.make_async_remote_copy(
            src_ref=src, dst_ref=dst, send_sem=send, recv_sem=recv, device_id=device, device_id_type=MESH)

    def natural(place):
        return RADIX * jnp.bitwise_and(place, per - 1) + lax.shift_right_logical(place, per.bit_length() - 1)

    def rows_of(member):
        return gall.at[pl.ds(pl.multiple_of(member * own_rows, own_rows), own_rows)]

    def gain_copy(a, e, member):
        rel = a * cores + e
        to = at(a, 0)[0] if e == 0 else at(0, e)[0]
        return remote(rows_of(member), rows_of(member), gsems.at[rel], grecv.at[rel], to)

    place = lax.broadcasted_iota(jnp.int32, (window, 1), 0)
    column = natural(lax.broadcasted_iota(jnp.int32, (1, window), 1))
    order = jnp.where(place == column, 1.0, 0.0).astype(BF16)
    gain_load.wait()
    gain = own[...]
    high = gain.astype(BF16)
    low = (gain - high.astype(F32)).astype(BF16)
    gain = jnp.dot(high, order, preferred_element_type=F32) + jnp.dot(low, order, preferred_element_type=F32)
    gall[pl.ds(pl.multiple_of(me * own_rows, own_rows), own_rows), :] = (gain * LEVELS + 0.5).astype(jnp.int16)

    pl.semaphore_wait(barrier, chips * cores - 1 + len(HOPS))
    gain_copies = [gain_copy(a, 0, me) for a in range(1, chips)] + [gain_copy(0, e, me) for e in range(1, cores)]
    for c in gain_copies:
        c.start()

    down = taps(shift_ref[0, 0])
    across = taps(shift_ref[0, 1])

    def filter_rows(x):
        total = down[0] * x
        for d in range(1, 4):
            total += down[d] * pltpu.roll(x, window - d, 0)
        return total

    def rounded(tap):
        return jnp.full((1, S), tap, F32).astype(BF16).astype(F32)

    tops = [rounded(tap) for tap in across]
    rests = [tap - top for tap, top in zip(across, tops)]
    source = natural(place) - lax.broadcasted_iota(jnp.int32, (window, S), 1)
    for k in range(count):
        gap = source - offs_ref[0, 1, k]
        top = jnp.zeros((window, S), F32)
        rest = top
        for d in range(4):
            hit = gap == d
            top = jnp.where(hit, tops[d], top)
            rest = jnp.where(hit, rests[d], rest)
        mats[0, k] = top.astype(BF16)
        mats[1, k] = rest.astype(BF16)

    def columns(i, carry):
        load(i).wait()
        span = pl.ds(pl.multiple_of(i * step, step), step)
        a = [buf[0, span, j * fold:(j + 1) * fold] for j in range(RADIX)]
        b = [buf[1, span, j * fold:(j + 1) * fold] for j in range(RADIX)]
        ap, am, aq, an = a[0] + a[2], a[0] - a[2], a[1] + a[3], a[1] - a[3]
        bp, bm, bq, bn = b[0] + b[2], b[0] - b[2], b[1] + b[3], b[1] - b[3]
        folded = (
            (ap + aq, bp + bq),
            (am - bn, bm + an),
            (ap - aq, bp - bq),
            (am + bn, bm - an),
        )
        for c in range(RADIX):
            z = jnp.concatenate(folded[c], axis=0)
            high = z.astype(BF16)
            low = (z - high.astype(F32)).astype(BF16)
            out = jnp.dot(high, col_ref[0, c], preferred_element_type=F32)
            out += jnp.dot(low, col_ref[0, c], preferred_element_type=F32)
            out += jnp.dot(high, col_ref[1, c], preferred_element_type=F32)
            real = (out[:step, :per] - out[step:, per:]).astype(BF16)
            imag = (out[:step, per:] + out[step:, :per]).astype(BF16)
            spec[span, c * per:(c + 1) * per] = real
            spec[pl.ds(pl.multiple_of(rows + i * step, step), step), c * per:(c + 1) * per] = imag
        return carry

    col_load.wait()
    lax.fori_loop(0, chunks // 2, columns, 0)
    row_load.wait()
    cos = row_ref[0].astype(F32)
    sin = row_ref[1].astype(F32)
    if quarter:
        turn = jnp.bitwise_and(me * place, 3)
        plus = jnp.where(turn == 0, 1.0, jnp.where(turn == 2, -1.0, 0.0))
        cross = jnp.where(turn == 1, 1.0, jnp.where(turn == 3, -1.0, 0.0))
        cos, sin = plus * cos - cross * sin, cross * cos + plus * sin
    table[:, :rows] = cos.astype(BF16)
    table[:, rows:] = (-sin).astype(BF16)
    lax.fori_loop(chunks // 2, chunks - 1, columns, 0)
    for a in range(1, chips):
        frm = at(-a, 0)[1]
        gain_copy(a, 0, frm).wait_recv()
        for e in range(1, cores):
            c = gain_copy(a, e, frm)
            c.start()
            gain_copies.append(c)
    lax.fori_loop(chunks - 1, chunks, columns, 0)

    for a in range(chips):
        for e in range(1, cores):
            gain_copy(a, e, at(-a, -e)[1]).wait_recv()
    scale = 1.0 / (LEVELS * length)
    half = window // 2
    for q in range(2):
        image = jnp.dot(table[...], spec[:, q * half:(q + 1) * half], preferred_element_type=F32)
        image = filter_rows(image * (gall[:, q * half:(q + 1) * half].astype(F32) * scale))
        for j in range(half // LANES):
            filt[q * half // LANES + j] = image[:, j * LANES:(j + 1) * LANES]

    def cropped(ref, start, size):
        return jnp.concatenate([ref[q, pl.ds(start, size), :] for q in range(window // LANES)], axis=1)

    core_copies = []
    for k in range(count):
        left = cropped(filt, offs_ref[0, 0, k], S).astype(BF16)
        piece = jnp.dot(left, mats[0, k], preferred_element_type=F32)
        piece += jnp.dot(left, mats[1, k], preferred_element_type=F32)
        for a in range(chips):
            for e in range(cores):
                m = a * cores + e
                pieces[k, e, a] = piece[m * side:(m + 1) * side]
                psend[k, e, a] = piece[m * side:(m + 1) * side].astype(BF16)
        for e in range(1, cores):
            to = lax.rem(core + e, cores)
            c = remote(psend.at[k, to], precv.at[e - 1, k], csems.at[e - 1, k], crecv.at[e - 1, k], at(0, e)[0])
            c.start()
            core_copies.append(c)

    def owed(terms, hop, slot):
        tile = lax.rem(owner + hop + owners, owners) * TILE_DEV + slot
        total = jnp.where(tiles_ref[owner, 0] == tile, 1.0, 0.0) * terms[0]
        for k in range(1, count):
            total += jnp.where(tiles_ref[owner, k] == tile, 1.0, 0.0) * terms[k]
        return total

    for q in range(window // LANES):
        g = gall[:, q * LANES:(q + 1) * LANES].astype(F32) * (1.0 / LEVELS)
        squares[q] = filter_rows(g * g)
    terms = []
    for k in range(count):
        den = cropped(squares, offs_ref[0, 0, k] + me * side, side)
        high = den.astype(BF16)
        low = (den - high.astype(F32)).astype(BF16)
        both = jnp.dot(jnp.concatenate([high, low], axis=0), mats[0, k], preferred_element_type=F32)
        terms.append(both[:side] + both[side:] + jnp.dot(high, mats[1, k], preferred_element_type=F32))
    den_copies = []
    for h, hop in enumerate(HOPS):
        for slot in range(TILE_DEV):
            dsend[h, slot] = owed(terms, hop, slot).astype(BF16)
        c = remote(dsend.at[h], drecv.at[h], dsems.at[h], drsems.at[h], beam(hop))
        c.start()
        den_copies.append(c)
    dens = [owed(terms, 0, slot) for slot in range(TILE_DEV)]

    for c in core_copies:
        c.wait_recv()

    def summed(k, to, p):
        span = slice(p * cut, (p + 1) * cut)
        total = pieces[k, core, to, span]
        for e in range(1, cores):
            total += precv[e - 1, k, to, span].astype(F32)
        return total

    x_copies = []
    for p in range(parts):
        for a in range(1, chips):
            to = lax.rem(chip + a, chips)
            for k in range(count):
                xsend[p, a - 1, k] = summed(k, to, p).astype(BF16)
            c = remote(xsend.at[p, a - 1], xrecv.at[p, a - 1], xsems.at[p, a - 1], xrsems.at[p, a - 1], at(a, 0)[0])
            c.start()
            x_copies.append(c)
    z_copies = []
    nums = []
    for p in range(parts):
        terms = [summed(k, chip, p) for k in range(count)]
        for a in range(1, chips):
            x_copies[p * (chips - 1) + a - 1].wait_recv()
            terms = [terms[k] + xrecv[p, a - 1, k].astype(F32) for k in range(count)]
        for h, hop in enumerate(HOPS):
            for slot in range(TILE_DEV):
                zsend[p, h, slot] = owed(terms, hop, slot).astype(BF16)
            c = remote(zsend.at[p, h], zrecv.at[p, h], zsems.at[p, h], zrsems.at[p, h], beam(hop))
            c.start()
            z_copies.append(c)
        nums.append([owed(terms, 0, slot) for slot in range(TILE_DEV)])
    for h, c in enumerate(den_copies):
        c.wait_recv()
        dens = [dens[slot] + drecv[h, slot].astype(F32) for slot in range(TILE_DEV)]
    for p in range(parts):
        for h in range(len(HOPS)):
            z_copies[p * len(HOPS) + h].wait_recv()
        for slot in range(TILE_DEV):
            num = nums[p][slot]
            for h in range(len(HOPS)):
                num += zrecv[p, h, slot].astype(F32)
            out_ref[slot, p * cut:(p + 1) * cut] = num / jnp.maximum(dens[slot][p * cut:(p + 1) * cut], 0.5)
    for c in gain_copies + core_copies + den_copies + x_copies + z_copies:
        c.wait_send()


def body(uv_grid, beam_gain, sub_pixel, intersection_tiles, tile_offsets):
    chips, cores = lax.axis_size("fft"), lax.axis_size("sub")
    members = chips * cores
    rows = uv_grid.shape[2]
    length = uv_grid.shape[3]
    own_rows = beam_gain.shape[1]
    window = beam_gain.shape[2]
    side = S // members
    count = tile_offsets.shape[1]
    quarter = RADIX * rows == length
    if quarter:
        row_table = jnp.asarray(row_tables(length, window, rows))
    else:
        member = lax.axis_index("fft") * lax.axis_size("sub") + lax.axis_index("sub")
        freq = member * rows + jnp.arange(rows, dtype=jnp.int32)
        place = jnp.arange(window, dtype=jnp.int32) - window // 2
        angle = jnp.mod(place[:, None] * freq[None, :], length).astype(F32) * (2.0 * np.pi / length)
        row_table = jnp.stack([jnp.cos(angle), jnp.sin(angle)]).astype(BF16)
    col_table = jnp.asarray(column_tables(length, window))
    step = min(128, rows)
    parts = PARTS
    cut = side // parts
    hops = len(HOPS)
    vmem = pl.BlockSpec(memory_space=pltpu.VMEM)
    smem = pl.BlockSpec(memory_space=pltpu.SMEM)
    anywhere = pl.BlockSpec(memory_space=pl.ANY)
    dma = pltpu.SemaphoreType.DMA
    return pl.pallas_call(
        functools.partial(kernel, quarter, step),
        out_shape=jax.ShapeDtypeStruct((TILE_DEV, side, S), F32),
        in_specs=[smem, smem, smem, anywhere, anywhere, anywhere, anywhere],
        out_specs=vmem,
        scratch_shapes=[
            pltpu.VMEM((2, rows, length), F32),
            pltpu.VMEM(col_table.shape, BF16),
            pltpu.VMEM(row_table.shape, BF16),
            pltpu.VMEM((window, 2 * rows), BF16),
            pltpu.VMEM((2 * rows, window), BF16),
            pltpu.VMEM((own_rows, window), F32),
            pltpu.VMEM((window, window), jnp.int16),
            pltpu.VMEM((window // LANES, window, LANES), F32),
            pltpu.VMEM((window // LANES, window, LANES), F32),
            pltpu.VMEM((2, count, window, S), BF16),
            pltpu.VMEM((count, cores, chips, side, S), F32),
            pltpu.VMEM((count, cores, chips, side, S), BF16),
            pltpu.VMEM((cores - 1, count, chips, side, S), BF16),
            pltpu.VMEM((parts, chips - 1, count, cut, S), BF16),
            pltpu.VMEM((parts, chips - 1, count, cut, S), BF16),
            pltpu.VMEM((parts, hops, TILE_DEV, cut, S), BF16),
            pltpu.VMEM((parts, hops, TILE_DEV, cut, S), BF16),
            pltpu.VMEM((hops, TILE_DEV, side, S), BF16),
            pltpu.VMEM((hops, TILE_DEV, side, S), BF16),
            dma((rows // step + 3,)),
            dma((members,)),
            dma((members,)),
            dma((cores - 1, count)),
            dma((cores - 1, count)),
            dma((parts, chips - 1)),
            dma((parts, chips - 1)),
            dma((parts, hops)),
            dma((parts, hops)),
            dma((hops,)),
            dma((hops,)),
        ],
        compiler_params=pltpu.CompilerParams(collective_id=0, has_side_effects=True),
    )(sub_pixel, intersection_tiles, jnp.swapaxes(tile_offsets, 1, 2), beam_gain, uv_grid, col_table, row_table)


def solution(mesh):
    placed = (
        P(("group", "beam"), None, ("fft", "sub"), None),
        P(("group", "beam"), ("fft", "sub"), None),
        P(("group", "beam"), None),
        P("group", None),
        P(("group", "beam"), None, None),
    )
    return jax.shard_map(
        body,
        mesh=mesh,
        in_specs=placed,
        out_specs=P(("group", "beam"), ("fft", "sub"), None),
        check_vma=False,
    )
```

```python
import functools
import math

import jax
import jax.numpy as jnp
import ml_dtypes
import numpy as np
from jax import lax
from jax.experimental import pallas as pl
from jax.experimental.pallas import tpu as pltpu
from jax.sharding import PartitionSpec as P

S = 256
TILE_DEV = 2
RADIX = 8
ROOT = math.sqrt(0.5)
HOPS = (2, 1, -1)
PARTS = 2
LEVELS = 32000.0
LANES = 128
MESH = pl.DeviceIdType.MESH
F32 = jnp.float32
BF16 = jnp.bfloat16


def turns(rows, cols, length):
    angle = np.mod(np.outer(rows, cols), length) * (2.0 * np.pi / length)
    return np.cos(angle), np.sin(angle)


def column_tables(length, window):
    fold = length // RADIX
    per = window // RADIX
    tables = []
    for c in range(RADIX):
        cos, sin = turns(np.arange(fold), RADIX * np.arange(per) + c - window // 2, length)
        full = np.concatenate([sin, cos] if c % 2 else [cos, sin], axis=1).astype(np.float32)
        high = full.astype(ml_dtypes.bfloat16)
        low = (full - high.astype(np.float32)).astype(ml_dtypes.bfloat16)
        tables.append(np.concatenate([high, low], axis=1))
    return np.stack(tables)


def row_tables(length, window, rows):
    cos, sin = turns(np.arange(window) - window // 2, np.arange(rows), length)
    return np.stack([cos, sin]).astype(np.float32).astype(ml_dtypes.bfloat16)


def near(a):
    return (1.5 * a - 2.5) * a * a + 1.0


def far(a):
    return ((-0.5 * a + 2.5) * a - 4.0) * a + 2.0


def taps(frac):
    return far(1.0 + frac), near(frac), near(1.0 - frac), far(2.0 - frac)


def kernel(
    quarter, step, shift_ref, tiles_ref, offs_ref, gain_hbm, uv_ref, col_hbm, row_hbm, out_ref,
    buf, col_ref, row_ref, table, spec, own, gall, filt, squares, mats, pieces, psend, precv,
    xsend, xrecv, zsend, zrecv, dsend, drecv,
    load_sems, gsems, grecv, csems, crecv, xsems, xrsems, zsems, zrsems, dsems, drsems,
):
    chip, core = lax.axis_index("fft"), lax.axis_index("sub")
    chips, cores = lax.axis_size("fft"), lax.axis_size("sub")
    me = chip * cores + core
    owner = lax.axis_index("beam")
    owners = lax.axis_size("beam")
    rows, length = buf.shape[1], buf.shape[2]
    fold = length // RADIX
    own_rows, window = own.shape
    per = window // RADIX
    side = pieces.shape[3]
    count = offs_ref.shape[2]
    chunks = rows // step
    parts = xsend.shape[0]
    cut = side // parts

    def load(i):
        span = pl.ds(pl.multiple_of(i * step, step), step)
        return pltpu.make_async_copy(uv_ref.at[0, :, span], buf.at[:, span], load_sems.at[i])

    gain_load = pltpu.make_async_copy(gain_hbm.at[0], own, load_sems.at[chunks])
    col_load = pltpu.make_async_copy(col_hbm, col_ref, load_sems.at[chunks + 1])
    row_load = pltpu.make_async_copy(row_hbm, row_ref, load_sems.at[chunks + 2])
    gain_load.start()
    col_load.start()
    for i in range(chunks):
        load(i).start()
    row_load.start()

    def beam(hop):
        return {"beam": lax.rem(owner + hop + owners, owners)}

    def at(a, e):
        other = lax.rem(chip + a + chips, chips), lax.rem(core + e + cores, cores)
        return {"fft": other[0], "sub": other[1]}, other[0] * cores + other[1]

    barrier = pltpu.get_barrier_semaphore()
    for a in range(chips):
        for e in range(cores):
            if a or e:
                pl.semaphore_signal(barrier, inc=1, device_id=at(a, e)[0], device_id_type=MESH)
    for hop in HOPS:
        pl.semaphore_signal(barrier, inc=1, device_id=beam(-hop), device_id_type=MESH)

    def remote(src, dst, send, recv, device):
        return pltpu.make_async_remote_copy(
            src_ref=src, dst_ref=dst, send_sem=send, recv_sem=recv, device_id=device, device_id_type=MESH)

    def natural(place):
        return RADIX * jnp.bitwise_and(place, per - 1) + lax.shift_right_logical(place, per.bit_length() - 1)

    def rows_of(member):
        return gall.at[pl.ds(pl.multiple_of(member * own_rows, own_rows), own_rows)]

    def gain_copy(a, e, member):
        rel = a * cores + e
        to = at(a, 0)[0] if e == 0 else at(0, e)[0]
        return remote(rows_of(member), rows_of(member), gsems.at[rel], grecv.at[rel], to)

    place = lax.broadcasted_iota(jnp.int32, (window, 1), 0)
    column = natural(lax.broadcasted_iota(jnp.int32, (1, window), 1))
    order = jnp.where(place == column, 1.0, 0.0).astype(BF16)
    gain_load.wait()
    gain = own[...]
    high = gain.astype(BF16)
    low = (gain - high.astype(F32)).astype(BF16)
    gain = jnp.dot(high, order, preferred_element_type=F32) + jnp.dot(low, order, preferred_element_type=F32)
    gall[pl.ds(pl.multiple_of(me * own_rows, own_rows), own_rows), :] = (gain * LEVELS + 0.5).astype(jnp.int16)

    pl.semaphore_wait(barrier, chips * cores - 1 + len(HOPS))
    gain_copies = [gain_copy(a, 0, me) for a in range(1, chips)] + [gain_copy(0, e, me) for e in range(1, cores)]
    for c in gain_copies:
        c.start()

    down = taps(shift_ref[0, 0])
    across = taps(shift_ref[0, 1])

    def filter_rows(x):
        total = down[0] * x
        for d in range(1, 4):
            total += down[d] * pltpu.roll(x, window - d, 0)
        return total

    def split(tap):
        tap = jnp.full((1, S), tap, F32)
        top = tap.astype(BF16)
        return top, (tap - top.astype(F32)).astype(BF16)

    split_taps = [split(tap) for tap in across]
    source = (natural(place) - lax.broadcasted_iota(jnp.int32, (window, S), 1)).astype(jnp.int16)
    for k in range(count):
        gap = source - jnp.full((1, S), offs_ref[0, 1, k], jnp.int32).astype(jnp.int16)
        top = jnp.zeros((window, S), BF16)
        rest = top
        for d in range(4):
            hit = gap == d
            top = jnp.where(hit, split_taps[d][0], top)
            rest = jnp.where(hit, split_taps[d][1], rest)
        mats[0, k] = top
        mats[1, k] = rest

    first = lax.broadcasted_iota(jnp.int32, (1, 2 * per), 1) < per

    def quartet(f):
        (a0, b0), (a1, b1), (a2, b2), (a3, b3) = f
        ap, am, aq, an = a0 + a2, a0 - a2, a1 + a3, a1 - a3
        bp, bm, bq, bn = b0 + b2, b0 - b2, b1 + b3, b1 - b3
        return (ap + aq, bp + bq), (am - bn, bm + an), (ap - aq, bp - bq), (am + bn, bm - an)

    def columns(i, carry):
        load(i).wait()
        span = pl.ds(pl.multiple_of(i * step, step), step)
        parts_of = [(buf[0, span, j * fold:(j + 1) * fold], buf[1, span, j * fold:(j + 1) * fold]) for j in range(RADIX)]
        even, odd = quartet(parts_of[0::2]), quartet(parts_of[1::2])
        turned = []
        for c, (x, y) in enumerate(odd):
            if c == 1:
                x, y = ROOT * (x - y), ROOT * (x + y)
            elif c == 2:
                x, y = -y, x
            elif c == 3:
                x, y = -ROOT * (x + y), ROOT * (x - y)
            turned.append((x, y))
        folded = [(e[0] + t[0], e[1] + t[1]) for e, t in zip(even, turned)]
        folded += [(e[0] - t[0], e[1] - t[1]) for e, t in zip(even, turned)]
        done = pl.ds(pl.multiple_of(rows + i * step, step), step)
        for c in range(0, RADIX, 2):
            pair = []
            for d in range(2):
                z = jnp.concatenate(folded[c + d], axis=0)
                high = z.astype(BF16)
                low = (z - high.astype(F32)).astype(BF16)
                out = jnp.dot(jnp.concatenate([high, low], axis=0), col_ref[c + d], preferred_element_type=F32)
                out = out[:2 * step] + out[2 * step:]
                out = out[:, :2 * per] + out[:, 2 * per:]
                swapped = pltpu.roll(out[step:], per, 1)
                pair.append(out[:step] + jnp.where(first, -swapped, swapped) if d == 0
                            else out[:step] + jnp.where(first, swapped, -swapped))
            real = jnp.where(first, pair[0], pair[1])
            imag = pltpu.roll(jnp.where(first, pair[1], pair[0]), per, 1)
            spec[span, c * per:(c + 2) * per] = real.astype(BF16)
            spec[done, c * per:(c + 2) * per] = imag.astype(BF16)
        return carry

    col_load.wait()
    lax.fori_loop(0, chunks // 2, columns, 0)
    row_load.wait()
    cos, sin = row_ref[0], row_ref[1]
    if quarter:
        turn = jnp.bitwise_and(me * place, 3)
        plus = jnp.where(turn == 0, 1.0, jnp.where(turn == 2, -1.0, 0.0))
        cross = jnp.where(turn == 1, 1.0, jnp.where(turn == 3, -1.0, 0.0))
        plus = jnp.broadcast_to(plus, (window, LANES)).astype(BF16)
        cross = jnp.broadcast_to(cross, (window, LANES)).astype(BF16)
        for q in range(rows // LANES):
            x, y = cos[:, q * LANES:(q + 1) * LANES], sin[:, q * LANES:(q + 1) * LANES]
            table[:, q * LANES:(q + 1) * LANES] = plus * x - cross * y
            table[:, rows + q * LANES:rows + (q + 1) * LANES] = -(cross * x + plus * y)
    else:
        table[:, :rows] = cos
        table[:, rows:] = -sin
    lax.fori_loop(chunks // 2, chunks - 1, columns, 0)
    for a in range(1, chips):
        frm = at(-a, 0)[1]
        gain_copy(a, 0, frm).wait_recv()
        for e in range(1, cores):
            c = gain_copy(a, e, frm)
            c.start()
            gain_copies.append(c)
    lax.fori_loop(chunks - 1, chunks, columns, 0)

    for a in range(chips):
        for e in range(1, cores):
            gain_copy(a, e, at(-a, -e)[1]).wait_recv()
    scale = 1.0 / (LEVELS * length)
    half = window // 2
    for q in range(2):
        image = jnp.dot(table[...], spec[:, q * half:(q + 1) * half], preferred_element_type=F32)
        image = filter_rows(image * (gall[:, q * half:(q + 1) * half].astype(F32) * scale))
        for j in range(half // LANES):
            filt[q * half // LANES + j] = image[:, j * LANES:(j + 1) * LANES]

    def cropped(ref, start, size):
        return jnp.concatenate([ref[q, pl.ds(start, size), :] for q in range(window // LANES)], axis=1)

    core_copies = []
    for k in range(count):
        left = cropped(filt, offs_ref[0, 0, k], S).astype(BF16)
        piece = jnp.dot(left, mats[0, k], preferred_element_type=F32)
        piece += jnp.dot(left, mats[1, k], preferred_element_type=F32)
        for a in range(chips):
            for e in range(cores):
                m = a * cores + e
                pieces[k, e, a] = piece[m * side:(m + 1) * side]
                psend[k, e, a] = piece[m * side:(m + 1) * side].astype(BF16)
        for e in range(1, cores):
            to = lax.rem(core + e, cores)
            c = remote(psend.at[k, to], precv.at[e - 1, k], csems.at[e - 1, k], crecv.at[e - 1, k], at(0, e)[0])
            c.start()
            core_copies.append(c)

    def owed(terms, hop, slot):
        tile = lax.rem(owner + hop + owners, owners) * TILE_DEV + slot
        total = jnp.where(tiles_ref[owner, 0] == tile, 1.0, 0.0) * terms[0]
        for k in range(1, count):
            total += jnp.where(tiles_ref[owner, k] == tile, 1.0, 0.0) * terms[k]
        return total

    for q in range(window // LANES):
        g = gall[:, q * LANES:(q + 1) * LANES].astype(F32) * (1.0 / LEVELS)
        squares[q] = filter_rows(g * g)
    terms = []
    for k in range(count):
        den = cropped(squares, offs_ref[0, 0, k] + me * side, side)
        high = den.astype(BF16)
        low = (den - high.astype(F32)).astype(BF16)
        both = jnp.dot(jnp.concatenate([high, low], axis=0), mats[0, k], preferred_element_type=F32)
        terms.append(both[:side] + both[side:] + jnp.dot(high, mats[1, k], preferred_element_type=F32))
    den_copies = []
    for h, hop in enumerate(HOPS):
        for slot in range(TILE_DEV):
            dsend[h, slot] = owed(terms, hop, slot).astype(BF16)
        c = remote(dsend.at[h], drecv.at[h], dsems.at[h], drsems.at[h], beam(hop))
        c.start()
        den_copies.append(c)
    dens = [owed(terms, 0, slot) for slot in range(TILE_DEV)]

    for c in core_copies:
        c.wait_recv()

    def summed(k, to, p):
        span = slice(p * cut, (p + 1) * cut)
        total = pieces[k, core, to, span]
        for e in range(1, cores):
            total += precv[e - 1, k, to, span].astype(F32)
        return total

    x_copies = []
    for p in range(parts):
        for a in range(1, chips):
            to = lax.rem(chip + a, chips)
            for k in range(count):
                xsend[p, a - 1, k] = summed(k, to, p).astype(BF16)
            c = remote(xsend.at[p, a - 1], xrecv.at[p, a - 1], xsems.at[p, a - 1], xrsems.at[p, a - 1], at(a, 0)[0])
            c.start()
            x_copies.append(c)
    z_copies = []
    nums = []
    for p in range(parts):
        terms = [summed(k, chip, p) for k in range(count)]
        for a in range(1, chips):
            x_copies[p * (chips - 1) + a - 1].wait_recv()
            terms = [terms[k] + xrecv[p, a - 1, k].astype(F32) for k in range(count)]
        for h, hop in enumerate(HOPS):
            for slot in range(TILE_DEV):
                zsend[p, h, slot] = owed(terms, hop, slot).astype(BF16)
            c = remote(zsend.at[p, h], zrecv.at[p, h], zsems.at[p, h], zrsems.at[p, h], beam(hop))
            c.start()
            z_copies.append(c)
        nums.append([owed(terms, 0, slot) for slot in range(TILE_DEV)])
    for h, c in enumerate(den_copies):
        c.wait_recv()
        dens = [dens[slot] + drecv[h, slot].astype(F32) for slot in range(TILE_DEV)]
    for p in range(parts):
        for h in range(len(HOPS)):
            z_copies[p * len(HOPS) + h].wait_recv()
        for slot in range(TILE_DEV):
            num = nums[p][slot]
            for h in range(len(HOPS)):
                num += zrecv[p, h, slot].astype(F32)
            out_ref[slot, p * cut:(p + 1) * cut] = num / jnp.maximum(dens[slot][p * cut:(p + 1) * cut], 0.5)
    for c in gain_copies + core_copies + den_copies + x_copies + z_copies:
        c.wait_send()


def body(uv_grid, beam_gain, sub_pixel, intersection_tiles, tile_offsets):
    chips, cores = lax.axis_size("fft"), lax.axis_size("sub")
    members = chips * cores
    rows = uv_grid.shape[2]
    length = uv_grid.shape[3]
    own_rows = beam_gain.shape[1]
    window = beam_gain.shape[2]
    side = S // members
    count = tile_offsets.shape[1]
    quarter = 4 * rows == length
    if quarter:
        row_table = jnp.asarray(row_tables(length, window, rows))
    else:
        member = lax.axis_index("fft") * lax.axis_size("sub") + lax.axis_index("sub")
        freq = member * rows + jnp.arange(rows, dtype=jnp.int32)
        place = jnp.arange(window, dtype=jnp.int32) - window // 2
        angle = jnp.mod(place[:, None] * freq[None, :], length).astype(F32) * (2.0 * np.pi / length)
        row_table = jnp.stack([jnp.cos(angle), jnp.sin(angle)]).astype(BF16)
    col_table = jnp.asarray(column_tables(length, window))
    step = min(128, rows)
    parts = PARTS
    cut = side // parts
    hops = len(HOPS)
    vmem = pl.BlockSpec(memory_space=pltpu.VMEM)
    smem = pl.BlockSpec(memory_space=pltpu.SMEM)
    anywhere = pl.BlockSpec(memory_space=pl.ANY)
    dma = pltpu.SemaphoreType.DMA
    return pl.pallas_call(
        functools.partial(kernel, quarter, step),
        out_shape=jax.ShapeDtypeStruct((TILE_DEV, side, S), F32),
        in_specs=[smem, smem, smem, anywhere, anywhere, anywhere, anywhere],
        out_specs=vmem,
        scratch_shapes=[
            pltpu.VMEM((2, rows, length), F32),
            pltpu.VMEM(col_table.shape, BF16),
            pltpu.VMEM(row_table.shape, BF16),
            pltpu.VMEM((window, 2 * rows), BF16),
            pltpu.VMEM((2 * rows, window), BF16),
            pltpu.VMEM((own_rows, window), F32),
            pltpu.VMEM((window, window), jnp.int16),
            pltpu.VMEM((window // LANES, window, LANES), F32),
            pltpu.VMEM((window // LANES, window, LANES), F32),
            pltpu.VMEM((2, count, window, S), BF16),
            pltpu.VMEM((count, cores, chips, side, S), F32),
            pltpu.VMEM((count, cores, chips, side, S), BF16),
            pltpu.VMEM((cores - 1, count, chips, side, S), BF16),
            pltpu.VMEM((parts, chips - 1, count, cut, S), BF16),
            pltpu.VMEM((parts, chips - 1, count, cut, S), BF16),
            pltpu.VMEM((parts, hops, TILE_DEV, cut, S), BF16),
            pltpu.VMEM((parts, hops, TILE_DEV, cut, S), BF16),
            pltpu.VMEM((hops, TILE_DEV, side, S), BF16),
            pltpu.VMEM((hops, TILE_DEV, side, S), BF16),
            dma((rows // step + 3,)),
            dma((members,)),
            dma((members,)),
            dma((cores - 1, count)),
            dma((cores - 1, count)),
            dma((parts, chips - 1)),
            dma((parts, chips - 1)),
            dma((parts, hops)),
            dma((parts, hops)),
            dma((hops,)),
            dma((hops,)),
        ],
        compiler_params=pltpu.CompilerParams(collective_id=0, has_side_effects=True),
    )(sub_pixel, intersection_tiles, jnp.swapaxes(tile_offsets, 1, 2), beam_gain, uv_grid, col_table, row_table)


def solution(mesh):
    placed = (
        P(("group", "beam"), None, ("fft", "sub"), None),
        P(("group", "beam"), ("fft", "sub"), None),
        P(("group", "beam"), None),
        P("group", None),
        P(("group", "beam"), None, None),
    )
    return jax.shard_map(
        body,
        mesh=mesh,
        in_specs=placed,
        out_specs=P(("group", "beam"), ("fft", "sub"), None),
        check_vma=False,
    )
```

```python
import functools
import math

import jax
import jax.numpy as jnp
import ml_dtypes
import numpy as np
from jax import lax
from jax.experimental import pallas as pl
from jax.experimental.pallas import tpu as pltpu
from jax.sharding import PartitionSpec as P

S = 256
TILE_DEV = 2
RADIX = 8
ROOT = math.sqrt(0.5)
HOPS = (2, 1, -1)
PARTS = 1
LEVELS = 32000.0
LANES = 128
PACK = 16
MESH = pl.DeviceIdType.MESH
F32 = jnp.float32
BF16 = jnp.bfloat16


def turns(rows, cols, length):
    angle = np.mod(np.outer(rows, cols), length) * (2.0 * np.pi / length)
    return np.cos(angle), np.sin(angle)


def column_tables(length, window):
    fold = length // RADIX
    per = window // RADIX
    tables = []
    for c in range(RADIX):
        cos, sin = turns(np.arange(fold), RADIX * np.arange(per) + c - window // 2, length)
        full = np.concatenate([sin, cos] if c % 2 else [cos, sin], axis=1).astype(np.float32)
        high = full.astype(ml_dtypes.bfloat16)
        low = (full - high.astype(np.float32)).astype(ml_dtypes.bfloat16)
        tables.append(np.concatenate([high, low], axis=1))
    return np.stack(tables)


def row_tables(length, window, rows):
    cos, sin = turns(np.arange(window) - window // 2, np.arange(rows), length)
    return np.stack([cos, sin]).astype(np.float32).astype(ml_dtypes.bfloat16)


def near(a):
    return (1.5 * a - 2.5) * a * a + 1.0


def far(a):
    return ((-0.5 * a + 2.5) * a - 4.0) * a + 2.0


def taps(frac):
    return far(1.0 + frac), near(frac), near(1.0 - frac), far(2.0 - frac)


def kernel(
    quarter, step, shift_ref, tiles_ref, offs_ref, gain_hbm, uv_ref, col_hbm, row_hbm, out_ref,
    buf, zbuf, col_ref, row_ref, table, spec, own, gall, filt, squares, mats, pieces, psend, precv,
    xsend, xrecv, zsend, zrecv, dsend, drecv,
    load_sems, gsems, grecv, csems, crecv, xsems, xrsems, zsems, zrsems, dsems, drsems,
):
    chip, core = lax.axis_index("fft"), lax.axis_index("sub")
    chips, cores = lax.axis_size("fft"), lax.axis_size("sub")
    me = chip * cores + core
    owner = lax.axis_index("beam")
    owners = lax.axis_size("beam")
    rows, length = buf.shape[1], buf.shape[2]
    fold = length // RADIX
    own_rows, window = own.shape
    per = window // RADIX
    side = pieces.shape[3]
    count = offs_ref.shape[2]
    chunks = rows // step
    parts = xsend.shape[0]
    cut = side // parts

    def load(i):
        span = pl.ds(pl.multiple_of(i * step, step), step)
        return pltpu.make_async_copy(uv_ref.at[0, :, span], buf.at[:, span], load_sems.at[i])

    gain_load = pltpu.make_async_copy(gain_hbm.at[0], own, load_sems.at[chunks])
    col_load = pltpu.make_async_copy(col_hbm, col_ref, load_sems.at[chunks + 1])
    row_load = pltpu.make_async_copy(row_hbm, row_ref, load_sems.at[chunks + 2])
    gain_load.start()
    col_load.start()
    for i in range(chunks):
        load(i).start()
    row_load.start()

    def beam(hop):
        return {"beam": lax.rem(owner + hop + owners, owners)}

    def at(a, e):
        other = lax.rem(chip + a + chips, chips), lax.rem(core + e + cores, cores)
        return {"fft": other[0], "sub": other[1]}, other[0] * cores + other[1]

    barrier = pltpu.get_barrier_semaphore()
    for a in range(chips):
        for e in range(cores):
            if a or e:
                pl.semaphore_signal(barrier, inc=1, device_id=at(a, e)[0], device_id_type=MESH)
    for hop in HOPS:
        pl.semaphore_signal(barrier, inc=1, device_id=beam(-hop), device_id_type=MESH)

    def remote(src, dst, send, recv, device):
        return pltpu.make_async_remote_copy(
            src_ref=src, dst_ref=dst, send_sem=send, recv_sem=recv, device_id=device, device_id_type=MESH)

    def natural(place):
        return RADIX * jnp.bitwise_and(place, per - 1) + lax.shift_right_logical(place, per.bit_length() - 1)

    def rows_of(member):
        return gall.at[pl.ds(pl.multiple_of(member * own_rows, own_rows), own_rows)]

    def gain_copy(a, e, member):
        rel = a * cores + e
        to = at(a, 0)[0] if e == 0 else at(0, e)[0]
        return remote(rows_of(member), rows_of(member), gsems.at[rel], grecv.at[rel], to)

    place = lax.broadcasted_iota(jnp.int32, (window, 1), 0)
    column = natural(lax.broadcasted_iota(jnp.int32, (1, window), 1))
    order = jnp.where(place == column, 1.0, 0.0).astype(BF16)
    gain_load.wait()
    gain = own[...]
    high = gain.astype(BF16)
    low = (gain - high.astype(F32)).astype(BF16)
    gain = jnp.dot(high, order, preferred_element_type=F32) + jnp.dot(low, order, preferred_element_type=F32)
    gall[pl.ds(pl.multiple_of(me * own_rows, own_rows), own_rows), :] = (gain * LEVELS + 0.5).astype(jnp.int16)

    pl.semaphore_wait(barrier, chips * cores - 1 + len(HOPS))
    gain_copies = [gain_copy(a, 0, me) for a in range(1, chips)] + [gain_copy(0, e, me) for e in range(1, cores)]
    for c in gain_copies:
        c.start()

    down = taps(shift_ref[0, 0])
    across = taps(shift_ref[0, 1])

    def filter_rows(x):
        total = down[0] * x
        for d in range(1, 4):
            total += down[d] * pltpu.roll(x, window - d, 0)
        return total

    def split(tap):
        tap = jnp.full((1, S), tap, F32)
        top = tap.astype(BF16)
        return top, (tap - top.astype(F32)).astype(BF16)

    split_taps = [split(tap) for tap in across]
    source = (natural(place) - lax.broadcasted_iota(jnp.int32, (window, S), 1)).astype(jnp.int16)
    for k in range(count):
        gap = source - jnp.full((1, S), offs_ref[0, 1, k], jnp.int32).astype(jnp.int16)
        top = jnp.zeros((window, S), BF16)
        rest = top
        for d in range(4):
            hit = gap == d
            top = jnp.where(hit, split_taps[d][0], top)
            rest = jnp.where(hit, split_taps[d][1], rest)
        mats[0, k] = top
        mats[1, k] = rest

    first = lax.broadcasted_iota(jnp.int32, (1, 2 * per), 1) < per

    def quartet(f):
        (a0, b0), (a1, b1), (a2, b2), (a3, b3) = f
        ap, am, aq, an = a0 + a2, a0 - a2, a1 + a3, a1 - a3
        bp, bm, bq, bn = b0 + b2, b0 - b2, b1 + b3, b1 - b3
        return (ap + aq, bp + bq), (am - bn, bm + an), (ap - aq, bp - bq), (am + bn, bm - an)

    def lanes_of(ref):
        return jnp.concatenate([ref[t] for t in range(ref.shape[0])], axis=1)

    def fold_rows(i, start, stop):
        for r in range(start, stop, PACK):
            for t in range(0, fold, LANES):
                span = slice(i * step + r, i * step + r + PACK)
                pieces_of = [tuple(buf[n, span, j * fold + t:j * fold + t + LANES] for n in range(2)) for j in range(RADIX)]
                even, odd = quartet(pieces_of[0::2]), quartet(pieces_of[1::2])
                for c in range(RADIX // 2):
                    x, y = odd[c]
                    if c == 1:
                        x, y = ROOT * (x - y), ROOT * (x + y)
                    elif c == 2:
                        x, y = -y, x
                    elif c == 3:
                        x, y = -ROOT * (x + y), ROOT * (x - y)
                    e, f = even[c]
                    for d, z in ((c, (e + x, f + y)), (c + RADIX // 2, (e - x, f - y))):
                        for n in range(2):
                            high = z[n].astype(BF16)
                            zbuf[i % 2, d, 0, t // LANES, n * step + r:n * step + r + PACK] = high
                            zbuf[i % 2, d, 1, t // LANES, n * step + r:n * step + r + PACK] = (
                                z[n] - high.astype(F32)).astype(BF16)

    def transform(i):
        for c in range(0, RADIX, 2):
            if i + 1 < chunks:
                fold_rows(i + 1, c * step // RADIX, (c + 2) * step // RADIX)
            pair = []
            for d in range(2):
                out = jnp.dot(lanes_of(zbuf.at[i % 2, c + d, 0]), col_ref[c + d], preferred_element_type=F32)
                out += jnp.dot(lanes_of(zbuf.at[i % 2, c + d, 1]), col_ref[c + d], preferred_element_type=F32)
                out = out[:, :2 * per] + out[:, 2 * per:]
                swapped = pltpu.roll(out[step:], per, 1)
                pair.append(out[:step] + jnp.where(first, -swapped, swapped) if d == 0
                            else out[:step] + jnp.where(first, swapped, -swapped))
            real = jnp.where(first, pair[0], pair[1])
            imag = pltpu.roll(jnp.where(first, pair[1], pair[0]), per, 1)
            spec[i * step:(i + 1) * step, c * per:(c + 2) * per] = real.astype(BF16)
            spec[rows + i * step:rows + (i + 1) * step, c * per:(c + 2) * per] = imag.astype(BF16)

    def forward():
        for a in range(1, chips):
            frm = at(-a, 0)[1]
            gain_copy(a, 0, frm).wait_recv()
            for e in range(1, cores):
                c = gain_copy(a, e, frm)
                c.start()
                gain_copies.append(c)

    def make_table():
        row_load.wait()
        cos, sin = row_ref[0], row_ref[1]
        if quarter:
            turn = jnp.bitwise_and(me * place, 3)
            plus = jnp.where(turn == 0, 1.0, jnp.where(turn == 2, -1.0, 0.0))
            cross = jnp.where(turn == 1, 1.0, jnp.where(turn == 3, -1.0, 0.0))
            plus = jnp.broadcast_to(plus, (window, LANES)).astype(BF16)
            cross = jnp.broadcast_to(cross, (window, LANES)).astype(BF16)
            for q in range(rows // LANES):
                x, y = cos[:, q * LANES:(q + 1) * LANES], sin[:, q * LANES:(q + 1) * LANES]
                table[:, q * LANES:(q + 1) * LANES] = plus * x - cross * y
                table[:, rows + q * LANES:rows + (q + 1) * LANES] = -(cross * x + plus * y)
        else:
            table[:, :rows] = cos
            table[:, rows:] = -sin

    load(0).wait()
    fold_rows(0, 0, step)
    col_load.wait()
    for i in range(chunks):
        if i + 1 < chunks:
            load(i + 1).wait()
        transform(i)
        if i == chunks - 2:
            make_table()
            forward()

    for a in range(chips):
        for e in range(1, cores):
            gain_copy(a, e, at(-a, -e)[1]).wait_recv()
    scale = 1.0 / (LEVELS * length)
    half = window // 2
    for q in range(2):
        image = jnp.dot(table[...], spec[:, q * half:(q + 1) * half], preferred_element_type=F32)
        image = filter_rows(image * (gall[:, q * half:(q + 1) * half].astype(F32) * scale))
        for j in range(half // LANES):
            filt[q * half // LANES + j] = image[:, j * LANES:(j + 1) * LANES]

    def cropped(ref, start, size):
        return jnp.concatenate([ref[q, pl.ds(start, size), :] for q in range(window // LANES)], axis=1)

    core_copies = []
    for k in range(count):
        left = cropped(filt, offs_ref[0, 0, k], S).astype(BF16)
        piece = jnp.dot(left, mats[0, k], preferred_element_type=F32)
        piece += jnp.dot(left, mats[1, k], preferred_element_type=F32)
        for a in range(chips):
            for e in range(cores):
                m = a * cores + e
                pieces[k, e, a] = piece[m * side:(m + 1) * side]
                psend[k, e, a] = piece[m * side:(m + 1) * side].astype(BF16)
        for e in range(1, cores):
            to = lax.rem(core + e, cores)
            c = remote(psend.at[k, to], precv.at[e - 1, k], csems.at[e - 1, k], crecv.at[e - 1, k], at(0, e)[0])
            c.start()
            core_copies.append(c)

    def owed(terms, hop, slot):
        tile = lax.rem(owner + hop + owners, owners) * TILE_DEV + slot
        total = jnp.where(tiles_ref[owner, 0] == tile, 1.0, 0.0) * terms[0]
        for k in range(1, count):
            total += jnp.where(tiles_ref[owner, k] == tile, 1.0, 0.0) * terms[k]
        return total

    for q in range(window // LANES):
        g = gall[:, q * LANES:(q + 1) * LANES].astype(F32) * (1.0 / LEVELS)
        squares[q] = filter_rows(g * g)
    terms = []
    for k in range(count):
        den = cropped(squares, offs_ref[0, 0, k] + me * side, side)
        high = den.astype(BF16)
        low = (den - high.astype(F32)).astype(BF16)
        both = jnp.dot(jnp.concatenate([high, low], axis=0), mats[0, k], preferred_element_type=F32)
        terms.append(both[:side] + both[side:] + jnp.dot(high, mats[1, k], preferred_element_type=F32))
    den_copies = []
    for h, hop in enumerate(HOPS):
        for slot in range(TILE_DEV):
            dsend[h, slot] = owed(terms, hop, slot).astype(BF16)
        c = remote(dsend.at[h], drecv.at[h], dsems.at[h], drsems.at[h], beam(hop))
        c.start()
        den_copies.append(c)
    dens = [owed(terms, 0, slot) for slot in range(TILE_DEV)]

    for c in core_copies:
        c.wait_recv()

    def summed(k, to, p):
        span = slice(p * cut, (p + 1) * cut)
        total = pieces[k, core, to, span]
        for e in range(1, cores):
            total += precv[e - 1, k, to, span].astype(F32)
        return total

    x_copies = []
    for p in range(parts):
        for a in range(1, chips):
            to = lax.rem(chip + a, chips)
            for k in range(count):
                xsend[p, a - 1, k] = summed(k, to, p).astype(BF16)
            c = remote(xsend.at[p, a - 1], xrecv.at[p, a - 1], xsems.at[p, a - 1], xrsems.at[p, a - 1], at(a, 0)[0])
            c.start()
            x_copies.append(c)
    z_copies = []
    nums = []
    for p in range(parts):
        terms = [summed(k, chip, p) for k in range(count)]
        for a in range(1, chips):
            x_copies[p * (chips - 1) + a - 1].wait_recv()
            terms = [terms[k] + xrecv[p, a - 1, k].astype(F32) for k in range(count)]
        for h, hop in enumerate(HOPS):
            for slot in range(TILE_DEV):
                zsend[p, h, slot] = owed(terms, hop, slot).astype(BF16)
            c = remote(zsend.at[p, h], zrecv.at[p, h], zsems.at[p, h], zrsems.at[p, h], beam(hop))
            c.start()
            z_copies.append(c)
        nums.append([owed(terms, 0, slot) for slot in range(TILE_DEV)])
    for h, c in enumerate(den_copies):
        c.wait_recv()
        dens = [dens[slot] + drecv[h, slot].astype(F32) for slot in range(TILE_DEV)]
    for p in range(parts):
        for h in range(len(HOPS)):
            z_copies[p * len(HOPS) + h].wait_recv()
        for slot in range(TILE_DEV):
            num = nums[p][slot]
            for h in range(len(HOPS)):
                num += zrecv[p, h, slot].astype(F32)
            out_ref[slot, p * cut:(p + 1) * cut] = num / jnp.maximum(dens[slot][p * cut:(p + 1) * cut], 0.5)
    for c in gain_copies + core_copies + den_copies + x_copies + z_copies:
        c.wait_send()


def body(uv_grid, beam_gain, sub_pixel, intersection_tiles, tile_offsets):
    chips, cores = lax.axis_size("fft"), lax.axis_size("sub")
    members = chips * cores
    rows = uv_grid.shape[2]
    length = uv_grid.shape[3]
    own_rows = beam_gain.shape[1]
    window = beam_gain.shape[2]
    side = S // members
    count = tile_offsets.shape[1]
    quarter = 4 * rows == length
    if quarter:
        row_table = jnp.asarray(row_tables(length, window, rows))
    else:
        member = lax.axis_index("fft") * lax.axis_size("sub") + lax.axis_index("sub")
        freq = member * rows + jnp.arange(rows, dtype=jnp.int32)
        place = jnp.arange(window, dtype=jnp.int32) - window // 2
        angle = jnp.mod(place[:, None] * freq[None, :], length).astype(F32) * (2.0 * np.pi / length)
        row_table = jnp.stack([jnp.cos(angle), jnp.sin(angle)]).astype(BF16)
    col_table = jnp.asarray(column_tables(length, window))
    step = min(128, rows)
    parts = PARTS
    cut = side // parts
    hops = len(HOPS)
    vmem = pl.BlockSpec(memory_space=pltpu.VMEM)
    smem = pl.BlockSpec(memory_space=pltpu.SMEM)
    anywhere = pl.BlockSpec(memory_space=pl.ANY)
    dma = pltpu.SemaphoreType.DMA
    return pl.pallas_call(
        functools.partial(kernel, quarter, step),
        out_shape=jax.ShapeDtypeStruct((TILE_DEV, side, S), F32),
        in_specs=[smem, smem, smem, anywhere, anywhere, anywhere, anywhere],
        out_specs=vmem,
        scratch_shapes=[
            pltpu.VMEM((2, rows, length), F32),
            pltpu.VMEM((2, RADIX, 2, length // RADIX // LANES, 2 * step, LANES), BF16),
            pltpu.VMEM(col_table.shape, BF16),
            pltpu.VMEM(row_table.shape, BF16),
            pltpu.VMEM((window, 2 * rows), BF16),
            pltpu.VMEM((2 * rows, window), BF16),
            pltpu.VMEM((own_rows, window), F32),
            pltpu.VMEM((window, window), jnp.int16),
            pltpu.VMEM((window // LANES, window, LANES), F32),
            pltpu.VMEM((window // LANES, window, LANES), F32),
            pltpu.VMEM((2, count, window, S), BF16),
            pltpu.VMEM((count, cores, chips, side, S), F32),
            pltpu.VMEM((count, cores, chips, side, S), BF16),
            pltpu.VMEM((cores - 1, count, chips, side, S), BF16),
            pltpu.VMEM((parts, chips - 1, count, cut, S), BF16),
            pltpu.VMEM((parts, chips - 1, count, cut, S), BF16),
            pltpu.VMEM((parts, hops, TILE_DEV, cut, S), BF16),
            pltpu.VMEM((parts, hops, TILE_DEV, cut, S), BF16),
            pltpu.VMEM((hops, TILE_DEV, side, S), BF16),
            pltpu.VMEM((hops, TILE_DEV, side, S), BF16),
            dma((rows // step + 3,)),
            dma((members,)),
            dma((members,)),
            dma((cores - 1, count)),
            dma((cores - 1, count)),
            dma((parts, chips - 1)),
            dma((parts, chips - 1)),
            dma((parts, hops)),
            dma((parts, hops)),
            dma((hops,)),
            dma((hops,)),
        ],
        compiler_params=pltpu.CompilerParams(collective_id=0, has_side_effects=True),
    )(sub_pixel, intersection_tiles, jnp.swapaxes(tile_offsets, 1, 2), beam_gain, uv_grid, col_table, row_table)


def solution(mesh):
    placed = (
        P(("group", "beam"), None, ("fft", "sub"), None),
        P(("group", "beam"), ("fft", "sub"), None),
        P(("group", "beam"), None),
        P("group", None),
        P(("group", "beam"), None, None),
    )
    return jax.shard_map(
        body,
        mesh=mesh,
        in_specs=placed,
        out_specs=P(("group", "beam"), ("fft", "sub"), None),
        check_vma=False,
    )
```

```python
import functools
import math

import jax
import jax.numpy as jnp
import ml_dtypes
import numpy as np
from jax import lax
from jax.experimental import pallas as pl
from jax.experimental.pallas import tpu as pltpu
from jax.sharding import PartitionSpec as P

S = 256
TILE_DEV = 2
RADIX = 8
ROOT = math.sqrt(0.5)
HOPS = (2, 1, -1)
PARTS = 1
LEVELS = 32000.0
LANES = 128
PACK = 16
MESH = pl.DeviceIdType.MESH
F32 = jnp.float32
BF16 = jnp.bfloat16


def turns(rows, cols, length):
    angle = np.mod(np.outer(rows, cols), length) * (2.0 * np.pi / length)
    return np.cos(angle), np.sin(angle)


def column_tables(length, window):
    fold = length // RADIX
    per = window // RADIX
    tables = []
    for c in range(RADIX):
        cos, sin = turns(np.arange(fold), RADIX * np.arange(per) + c - window // 2, length)
        full = np.concatenate([sin, cos] if c % 2 else [cos, sin], axis=1).astype(np.float32)
        high = full.astype(ml_dtypes.bfloat16)
        low = (full - high.astype(np.float32)).astype(ml_dtypes.bfloat16)
        tables.append(np.concatenate([high, low], axis=1))
    return np.stack(tables)


def row_tables(length, window, rows):
    cos, sin = turns(np.arange(window) - window // 2, np.arange(rows), length)
    return np.stack([cos, sin]).astype(np.float32).astype(ml_dtypes.bfloat16)


def near(a):
    return (1.5 * a - 2.5) * a * a + 1.0


def far(a):
    return ((-0.5 * a + 2.5) * a - 4.0) * a + 2.0


def taps(frac):
    return far(1.0 + frac), near(frac), near(1.0 - frac), far(2.0 - frac)


def kernel(
    quarter, step, shift_hbm, tiles_hbm, offs_hbm, gain_hbm, uv_ref, col_hbm, row_hbm, out_ref,
    shift_ref, tiles_ref, offs_ref, buf, zbuf, col_ref, row_ref, table, spec, own, gall, filt, squares, mats, pieces, psend, precv,
    xsend, xrecv, zsend, zrecv, dsend, drecv,
    load_sems, gsems, grecv, csems, crecv, xsems, xrsems, zsems, zrsems, dsems, drsems,
):
    chip, core = lax.axis_index("fft"), lax.axis_index("sub")
    chips, cores = lax.axis_size("fft"), lax.axis_size("sub")
    me = chip * cores + core
    owner = lax.axis_index("beam")
    owners = lax.axis_size("beam")
    rows, length = buf.shape[1], buf.shape[2]
    fold = length // RADIX
    own_rows, window = own.shape
    per = window // RADIX
    side = pieces.shape[3]
    count = offs_ref.shape[2]
    chunks = rows // step
    parts = xsend.shape[0]
    cut = side // parts

    def load(i):
        span = pl.ds(pl.multiple_of(i * step, step), step)
        return pltpu.make_async_copy(uv_ref.at[0, :, span], buf.at[:, span], load_sems.at[i])

    gain_load = pltpu.make_async_copy(gain_hbm.at[0], own, load_sems.at[chunks])
    col_load = pltpu.make_async_copy(col_hbm, col_ref, load_sems.at[chunks + 1])
    row_load = pltpu.make_async_copy(row_hbm, row_ref, load_sems.at[chunks + 2])
    small_loads = [
        pltpu.make_async_copy(src, dst, load_sems.at[chunks + 3 + n])
        for n, (src, dst) in enumerate(((shift_hbm, shift_ref), (tiles_hbm, tiles_ref), (offs_hbm, offs_ref)))]
    gain_load.start()
    for c in small_loads:
        c.start()
    col_load.start()
    for i in range(chunks):
        load(i).start()
    row_load.start()

    def beam(hop):
        return {"beam": lax.rem(owner + hop + owners, owners)}

    def at(a, e):
        other = lax.rem(chip + a + chips, chips), lax.rem(core + e + cores, cores)
        return {"fft": other[0], "sub": other[1]}, other[0] * cores + other[1]

    barrier = pltpu.get_barrier_semaphore()
    for a in range(chips):
        for e in range(cores):
            if a or e:
                pl.semaphore_signal(barrier, inc=1, device_id=at(a, e)[0], device_id_type=MESH)
    for hop in HOPS:
        pl.semaphore_signal(barrier, inc=1, device_id=beam(-hop), device_id_type=MESH)

    def remote(src, dst, send, recv, device):
        return pltpu.make_async_remote_copy(
            src_ref=src, dst_ref=dst, send_sem=send, recv_sem=recv, device_id=device, device_id_type=MESH)

    def natural(place):
        return RADIX * jnp.bitwise_and(place, per - 1) + lax.shift_right_logical(place, per.bit_length() - 1)

    def rows_of(member):
        return gall.at[pl.ds(pl.multiple_of(member * own_rows, own_rows), own_rows)]

    def gain_copy(a, e, member):
        rel = a * cores + e
        to = at(a, 0)[0] if e == 0 else at(0, e)[0]
        return remote(rows_of(member), rows_of(member), gsems.at[rel], grecv.at[rel], to)

    place = lax.broadcasted_iota(jnp.int32, (window, 1), 0)
    column = natural(lax.broadcasted_iota(jnp.int32, (1, window), 1))
    order = jnp.where(place == column, 1.0, 0.0).astype(BF16)
    gain_load.wait()
    gain = own[...]
    high = gain.astype(BF16)
    low = (gain - high.astype(F32)).astype(BF16)
    gain = jnp.dot(high, order, preferred_element_type=F32) + jnp.dot(low, order, preferred_element_type=F32)
    gall[pl.ds(pl.multiple_of(me * own_rows, own_rows), own_rows), :] = (gain * LEVELS + 0.5).astype(jnp.int16)

    pl.semaphore_wait(barrier, chips * cores - 1 + len(HOPS))
    gain_copies = [gain_copy(a, 0, me) for a in range(1, chips)] + [gain_copy(0, e, me) for e in range(1, cores)]
    for c in gain_copies:
        c.start()

    for c in small_loads:
        c.wait()
    down = taps(shift_ref[0, 0])
    across = taps(shift_ref[0, 1])

    def filter_rows(x):
        total = down[0] * x
        for d in range(1, 4):
            total += down[d] * pltpu.roll(x, window - d, 0)
        return total

    def split(tap):
        tap = jnp.full((1, S), tap, F32)
        top = tap.astype(BF16)
        return top, (tap - top.astype(F32)).astype(BF16)

    split_taps = [split(tap) for tap in across]
    source = (natural(place) - lax.broadcasted_iota(jnp.int32, (window, S), 1)).astype(jnp.int16)
    for k in range(count):
        gap = source - jnp.full((1, S), offs_ref[0, 1, k], jnp.int32).astype(jnp.int16)
        top = jnp.zeros((window, S), BF16)
        rest = top
        for d in range(4):
            hit = gap == d
            top = jnp.where(hit, split_taps[d][0], top)
            rest = jnp.where(hit, split_taps[d][1], rest)
        mats[0, k] = top
        mats[1, k] = rest

    first = lax.broadcasted_iota(jnp.int32, (1, 2 * per), 1) < per

    def quartet(f):
        (a0, b0), (a1, b1), (a2, b2), (a3, b3) = f
        ap, am, aq, an = a0 + a2, a0 - a2, a1 + a3, a1 - a3
        bp, bm, bq, bn = b0 + b2, b0 - b2, b1 + b3, b1 - b3
        return (ap + aq, bp + bq), (am - bn, bm + an), (ap - aq, bp - bq), (am + bn, bm - an)

    def lanes_of(ref):
        return jnp.concatenate([ref[t] for t in range(ref.shape[0])], axis=1)

    def fold_rows(i, start, stop):
        for r in range(start, stop, PACK):
            for t in range(0, fold, LANES):
                span = slice(i * step + r, i * step + r + PACK)
                pieces_of = [tuple(buf[n, span, j * fold + t:j * fold + t + LANES] for n in range(2)) for j in range(RADIX)]
                even, odd = quartet(pieces_of[0::2]), quartet(pieces_of[1::2])
                for c in range(RADIX // 2):
                    x, y = odd[c]
                    if c == 1:
                        x, y = ROOT * (x - y), ROOT * (x + y)
                    elif c == 2:
                        x, y = -y, x
                    elif c == 3:
                        x, y = -ROOT * (x + y), ROOT * (x - y)
                    e, f = even[c]
                    for d, z in ((c, (e + x, f + y)), (c + RADIX // 2, (e - x, f - y))):
                        for n in range(2):
                            high = z[n].astype(BF16)
                            zbuf[i % 2, d, 0, t // LANES, n * step + r:n * step + r + PACK] = high
                            zbuf[i % 2, d, 1, t // LANES, n * step + r:n * step + r + PACK] = (
                                z[n] - high.astype(F32)).astype(BF16)

    def transform(i):
        for c in range(0, RADIX, 2):
            if i + 1 < chunks:
                fold_rows(i + 1, c * step // RADIX, (c + 2) * step // RADIX)
            pair = []
            for d in range(2):
                out = jnp.dot(lanes_of(zbuf.at[i % 2, c + d, 0]), col_ref[c + d], preferred_element_type=F32)
                out += jnp.dot(lanes_of(zbuf.at[i % 2, c + d, 1]), col_ref[c + d], preferred_element_type=F32)
                out = out[:, :2 * per] + out[:, 2 * per:]
                swapped = pltpu.roll(out[step:], per, 1)
                pair.append(out[:step] + jnp.where(first, -swapped, swapped) if d == 0
                            else out[:step] + jnp.where(first, swapped, -swapped))
            real = jnp.where(first, pair[0], pair[1])
            imag = pltpu.roll(jnp.where(first, pair[1], pair[0]), per, 1)
            spec[i * step:(i + 1) * step, c * per:(c + 2) * per] = real.astype(BF16)
            spec[rows + i * step:rows + (i + 1) * step, c * per:(c + 2) * per] = imag.astype(BF16)

    def forward():
        for a in range(1, chips):
            frm = at(-a, 0)[1]
            gain_copy(a, 0, frm).wait_recv()
            for e in range(1, cores):
                c = gain_copy(a, e, frm)
                c.start()
                gain_copies.append(c)

    def make_table():
        row_load.wait()
        cos, sin = row_ref[0], row_ref[1]
        if quarter:
            turn = jnp.bitwise_and(me * place, 3)
            plus = jnp.where(turn == 0, 1.0, jnp.where(turn == 2, -1.0, 0.0))
            cross = jnp.where(turn == 1, 1.0, jnp.where(turn == 3, -1.0, 0.0))
            plus = jnp.broadcast_to(plus, (window, LANES)).astype(BF16)
            cross = jnp.broadcast_to(cross, (window, LANES)).astype(BF16)
            for q in range(rows // LANES):
                x, y = cos[:, q * LANES:(q + 1) * LANES], sin[:, q * LANES:(q + 1) * LANES]
                table[:, q * LANES:(q + 1) * LANES] = plus * x - cross * y
                table[:, rows + q * LANES:rows + (q + 1) * LANES] = -(cross * x + plus * y)
        else:
            table[:, :rows] = cos
            table[:, rows:] = -sin

    load(0).wait()
    fold_rows(0, 0, step)
    col_load.wait()
    for i in range(chunks):
        if i + 1 < chunks:
            load(i + 1).wait()
        transform(i)
        if i == chunks - 2:
            make_table()
            forward()

    for a in range(chips):
        for e in range(1, cores):
            gain_copy(a, e, at(-a, -e)[1]).wait_recv()
    scale = 1.0 / (LEVELS * length)
    half = window // 2
    for q in range(2):
        image = jnp.dot(table[...], spec[:, q * half:(q + 1) * half], preferred_element_type=F32)
        image = filter_rows(image * (gall[:, q * half:(q + 1) * half].astype(F32) * scale))
        for j in range(half // LANES):
            filt[q * half // LANES + j] = image[:, j * LANES:(j + 1) * LANES]

    def cropped(ref, start, size):
        return jnp.concatenate([ref[q, pl.ds(start, size), :] for q in range(window // LANES)], axis=1)

    core_copies = []
    for k in range(count):
        left = cropped(filt, offs_ref[0, 0, k], S).astype(BF16)
        piece = jnp.dot(left, mats[0, k], preferred_element_type=F32)
        piece += jnp.dot(left, mats[1, k], preferred_element_type=F32)
        for a in range(chips):
            for e in range(cores):
                m = a * cores + e
                pieces[k, e, a] = piece[m * side:(m + 1) * side]
                psend[e, k, a] = piece[m * side:(m + 1) * side].astype(BF16)
    for e in range(1, cores):
        to = lax.rem(core + e, cores)
        c = remote(psend.at[to], precv.at[e - 1], csems.at[e - 1], crecv.at[e - 1], at(0, e)[0])
        c.start()
        core_copies.append(c)

    def owed(terms, hop, slot):
        tile = lax.rem(owner + hop + owners, owners) * TILE_DEV + slot
        total = jnp.where(tiles_ref[owner, 0] == tile, 1.0, 0.0) * terms[0]
        for k in range(1, count):
            total += jnp.where(tiles_ref[owner, k] == tile, 1.0, 0.0) * terms[k]
        return total

    for q in range(window // LANES):
        g = gall[:, q * LANES:(q + 1) * LANES].astype(F32) * (1.0 / LEVELS)
        squares[q] = filter_rows(g * g)
    terms = []
    for k in range(count):
        den = cropped(squares, offs_ref[0, 0, k] + me * side, side)
        high = den.astype(BF16)
        low = (den - high.astype(F32)).astype(BF16)
        both = jnp.dot(jnp.concatenate([high, low], axis=0), mats[0, k], preferred_element_type=F32)
        terms.append(both[:side] + both[side:] + jnp.dot(high, mats[1, k], preferred_element_type=F32))
    den_copies = []
    for h, hop in enumerate(HOPS):
        for slot in range(TILE_DEV):
            dsend[h, slot] = owed(terms, hop, slot).astype(BF16)
        c = remote(dsend.at[h], drecv.at[h], dsems.at[h], drsems.at[h], beam(hop))
        c.start()
        den_copies.append(c)
    dens = [owed(terms, 0, slot) for slot in range(TILE_DEV)]

    for c in core_copies:
        c.wait_recv()

    def summed(k, to, p):
        span = slice(p * cut, (p + 1) * cut)
        total = pieces[k, core, to, span]
        for e in range(1, cores):
            total += precv[e - 1, k, to, span].astype(F32)
        return total

    x_copies = []
    for p in range(parts):
        for a in range(1, chips):
            to = lax.rem(chip + a, chips)
            for k in range(count):
                xsend[p, a - 1, k] = summed(k, to, p).astype(BF16)
            c = remote(xsend.at[p, a - 1], xrecv.at[p, a - 1], xsems.at[p, a - 1], xrsems.at[p, a - 1], at(a, 0)[0])
            c.start()
            x_copies.append(c)
    z_copies = []
    nums = []
    for p in range(parts):
        terms = [summed(k, chip, p) for k in range(count)]
        for a in range(1, chips):
            x_copies[p * (chips - 1) + a - 1].wait_recv()
            terms = [terms[k] + xrecv[p, a - 1, k].astype(F32) for k in range(count)]
        for h, hop in enumerate(HOPS):
            for slot in range(TILE_DEV):
                zsend[p, h, slot] = owed(terms, hop, slot).astype(BF16)
            c = remote(zsend.at[p, h], zrecv.at[p, h], zsems.at[p, h], zrsems.at[p, h], beam(hop))
            c.start()
            z_copies.append(c)
        nums.append([owed(terms, 0, slot) for slot in range(TILE_DEV)])
    for h, c in enumerate(den_copies):
        c.wait_recv()
        dens = [dens[slot] + drecv[h, slot].astype(F32) for slot in range(TILE_DEV)]
    for p in range(parts):
        for h in range(len(HOPS)):
            z_copies[p * len(HOPS) + h].wait_recv()
        for slot in range(TILE_DEV):
            num = nums[p][slot]
            for h in range(len(HOPS)):
                num += zrecv[p, h, slot].astype(F32)
            out_ref[slot, p * cut:(p + 1) * cut] = num / jnp.maximum(dens[slot][p * cut:(p + 1) * cut], 0.5)
    for c in gain_copies + core_copies + den_copies + x_copies + z_copies:
        c.wait_send()


def body(uv_grid, beam_gain, sub_pixel, intersection_tiles, tile_offsets):
    chips, cores = lax.axis_size("fft"), lax.axis_size("sub")
    members = chips * cores
    rows = uv_grid.shape[2]
    length = uv_grid.shape[3]
    own_rows = beam_gain.shape[1]
    window = beam_gain.shape[2]
    side = S // members
    count = tile_offsets.shape[1]
    quarter = 4 * rows == length
    if quarter:
        row_table = jnp.asarray(row_tables(length, window, rows))
    else:
        member = lax.axis_index("fft") * lax.axis_size("sub") + lax.axis_index("sub")
        freq = member * rows + jnp.arange(rows, dtype=jnp.int32)
        place = jnp.arange(window, dtype=jnp.int32) - window // 2
        angle = jnp.mod(place[:, None] * freq[None, :], length).astype(F32) * (2.0 * np.pi / length)
        row_table = jnp.stack([jnp.cos(angle), jnp.sin(angle)]).astype(BF16)
    col_table = jnp.asarray(column_tables(length, window))
    step = min(128, rows)
    parts = PARTS
    cut = side // parts
    hops = len(HOPS)
    vmem = pl.BlockSpec(memory_space=pltpu.VMEM)
    anywhere = pl.BlockSpec(memory_space=pl.ANY)
    dma = pltpu.SemaphoreType.DMA
    return pl.pallas_call(
        functools.partial(kernel, quarter, step),
        out_shape=jax.ShapeDtypeStruct((TILE_DEV, side, S), F32),
        in_specs=[anywhere] * 7,
        out_specs=vmem,
        scratch_shapes=[
            pltpu.SMEM(sub_pixel.shape, F32),
            pltpu.SMEM(intersection_tiles.shape, jnp.int32),
            pltpu.SMEM((1, 2, count), jnp.int32),
            pltpu.VMEM((2, rows, length), F32),
            pltpu.VMEM((2, RADIX, 2, length // RADIX // LANES, 2 * step, LANES), BF16),
            pltpu.VMEM(col_table.shape, BF16),
            pltpu.VMEM(row_table.shape, BF16),
            pltpu.VMEM((window, 2 * rows), BF16),
            pltpu.VMEM((2 * rows, window), BF16),
            pltpu.VMEM((own_rows, window), F32),
            pltpu.VMEM((window, window), jnp.int16),
            pltpu.VMEM((window // LANES, window, LANES), F32),
            pltpu.VMEM((window // LANES, window, LANES), F32),
            pltpu.VMEM((2, count, window, S), BF16),
            pltpu.VMEM((count, cores, chips, side, S), F32),
            pltpu.VMEM((cores, count, chips, side, S), BF16),
            pltpu.VMEM((cores - 1, count, chips, side, S), BF16),
            pltpu.VMEM((parts, chips - 1, count, cut, S), BF16),
            pltpu.VMEM((parts, chips - 1, count, cut, S), BF16),
            pltpu.VMEM((parts, hops, TILE_DEV, cut, S), BF16),
            pltpu.VMEM((parts, hops, TILE_DEV, cut, S), BF16),
            pltpu.VMEM((hops, TILE_DEV, side, S), BF16),
            pltpu.VMEM((hops, TILE_DEV, side, S), BF16),
            dma((rows // step + 6,)),
            dma((members,)),
            dma((members,)),
            dma((cores - 1,)),
            dma((cores - 1,)),
            dma((parts, chips - 1)),
            dma((parts, chips - 1)),
            dma((parts, hops)),
            dma((parts, hops)),
            dma((hops,)),
            dma((hops,)),
        ],
        compiler_params=pltpu.CompilerParams(collective_id=0, has_side_effects=True),
    )(sub_pixel, intersection_tiles, jnp.swapaxes(tile_offsets, 1, 2), beam_gain, uv_grid, col_table, row_table)


def solution(mesh):
    placed = (
        P(("group", "beam"), None, ("fft", "sub"), None),
        P(("group", "beam"), ("fft", "sub"), None),
        P(("group", "beam"), None),
        P("group", None),
        P(("group", "beam"), None, None),
    )
    return jax.shard_map(
        body,
        mesh=mesh,
        in_specs=placed,
        out_specs=P(("group", "beam"), ("fft", "sub"), None),
        check_vma=False,
    )
```
